32 devices in a mesh: row: 8 (over z, core), col: 4 (over y, x).
Axes of the slice: x: 2, y: 2, z: 4, core: 2. Of those that a mesh axis runs over, the one named last changes fastest.
Arguments:
- start_panel: bfloat16 [32768, 128], P(('col', 'row')), may hold values from -6 to 6
- block_values: bfloat16 [8, 4, 352, 128, 128], P('row', 'col'), may hold values from -0.078125 to 0.078125
- block_rows: int32 [8, 4, 352], P('row', 'col'), may hold values from 0 to 31, as said below
- block_cols: int32 [8, 4, 352], P('row', 'col'), may hold values from 0 to 63, as said below
- block_counts: int32 [8, 4], P('row', 'col'), may hold values from 141 to 352, as said below
Outputs:
- left_panel: bfloat16 [32768, 128], P(('row', 'col'))
- right_panel: bfloat16 [32768, 128], P(('col', 'row'))
The draws below stay inside these ranges and needn't reach their ends.
Inputs may be any that keep to these rules, and one draw needn't show every extreme that they name: `block_rows`: block rows lie in 0 to 31 within each tile; low block rows hold more blocks; in every tile some live slot names block row 31. `block_cols`: in every tile some live slot names block column 63; a position may repeat. Only the first block_counts[r, c] slots of tile (r, c) are live; some tile fills all 352 slots.
All inputs are finite; a program needn't handle non-finite values.
Results may differ from the reference program's by a relative error of at most 0.0085.
Values may be sent and summed in bfloat16 or wider, within the bound.
No kernel may reach another device: no remote copies, remote signals or barrier semaphores. Data moves between devices by JAX's collectives and lax.ppermute only.
A program may use at most 128 MiB of HBM per device.

```python
import jax
import jax.numpy as jnp
from jax import lax

BLK = 128
PANEL = 128
GROUP = 1024
KB = 352
NODES = 32768
BR = 32
BC = 64
N_ROW = 8
N_COL = 4


def draw_block_rows(key, part):
    first, second, third = jax.random.split(jax.random.fold_in(key, 11), 3)
    shape = (N_ROW, N_COL, KB)
    left = jax.random.randint(first, shape, 0, BR, dtype=jnp.int32)
    right = jax.random.randint(second, shape, 0, BR, dtype=jnp.int32)
    rows_drawn = left * right // BR
    placed = jax.random.randint(third, (N_ROW, N_COL, 1), 0, KB - 3 * KB // 5, dtype=jnp.int32)
    slots = jnp.arange(KB, dtype=jnp.int32)[None, None, :]
    return jnp.where(slots == placed, BR - 1, rows_drawn).astype(jnp.int32)


def draw_block_cols(key, part):
    first, third = jax.random.split(jax.random.fold_in(key, 23), 2)
    cols_drawn = jax.random.randint(first, (N_ROW, N_COL, KB), 0, BC, dtype=jnp.int32)
    placed = jax.random.randint(third, (N_ROW, N_COL, 1), 0, KB - 3 * KB // 5, dtype=jnp.int32)
    slots = jnp.arange(KB, dtype=jnp.int32)[None, None, :]
    return jnp.where(slots == placed, BC - 1, cols_drawn).astype(jnp.int32)


def draw_block_counts(key, part):
    first, second = jax.random.split(jax.random.fold_in(key, 37), 2)
    counts_drawn = KB - jax.random.randint(first, (N_ROW, N_COL), 0, 3 * KB // 5 + 1, dtype=jnp.int32)
    fullest = jax.random.randint(second, (), 0, N_ROW * N_COL, dtype=jnp.int32)
    tiles = jnp.arange(N_ROW * N_COL, dtype=jnp.int32).reshape(N_ROW, N_COL)
    return jnp.where(tiles == fullest, KB, counts_drawn).astype(jnp.int32)


def levels(own_key, extent, shards, least, largest):
    loudness = 1.0
    for position, shards_of in shards:
        steps = jax.random.uniform(jax.random.fold_in(jax.random.fold_in(own_key, 6), position), (shards_of,), jnp.float32, least / len(shards), largest / len(shards))
        loudness = loudness * jnp.repeat(jnp.exp(steps), extent[position] // shards_of).reshape((-1,) + (1,) * (len(extent) - 1 - position))
    return loudness


def normal_values(rng, dims, width, limit, cuts=(), kind=jnp.bfloat16):
    entries = width * jax.random.normal(rng, dims, jnp.float32)
    if cuts:
        entries = entries * levels(rng, dims, cuts, -0.22, 0.18)
    return jnp.clip(entries, -limit, limit).astype(kind)


def setup_inputs(seed: int = 0) -> dict:
    seeds = jax.random.split(jax.random.key(seed), 6)
    start_panel = normal_values(seeds[0], (NODES, PANEL), 1.0, 6.0, ((0, 32),))
    block_values = normal_values(seeds[1], (N_ROW, N_COL, KB, BLK, BLK), (KB * N_COL * BLK // BR) ** -0.5, 0.078125, ((0, 8), (1, 4)))
    block_rows = draw_block_rows(jax.random.fold_in(seeds[5], 71), 0)
    block_cols = draw_block_cols(jax.random.fold_in(seeds[5], 71), 0)
    block_counts = draw_block_counts(jax.random.fold_in(seeds[5], 71), 0)
    return dict(start_panel=start_panel, block_values=block_values, block_rows=block_rows, block_cols=block_cols, block_counts=block_counts)


def tile_product(values, index_out, index_in, live_count, panel_in, out_blocks, flipped):
    block_size = values.shape[-1]
    pieces = panel_in.reshape(-1, block_size, panel_in.shape[1])
    selected = jnp.take(pieces, index_in, axis=0).astype(jnp.float32)
    if flipped:
        products = jnp.einsum('kij,kip->kjp', values.astype(jnp.float32), selected)
    else:
        products = jnp.einsum('kij,kjp->kip', values.astype(jnp.float32), selected)
    live = (jnp.arange(values.shape[0]) < live_count).astype(jnp.float32)
    products = products * live[:, None, None]
    summed = jax.ops.segment_sum(products, index_out, num_segments=out_blocks)
    return summed.reshape(out_blocks * block_size, panel_in.shape[1])

def lower_cholesky(gram_total):
    order = gram_total.shape[0]
    positions = jnp.arange(order, dtype=jnp.int32)

    def column_step(index, lower):
        row_of = lax.dynamic_slice_in_dim(lower, index, 1, 0)[0]
        column = lax.dynamic_slice_in_dim(gram_total, index, 1, 1)[:, 0]
        column = column - jnp.dot(lower, row_of, precision=lax.Precision.HIGHEST)
        pivot = jnp.sqrt(lax.dynamic_slice_in_dim(column, index, 1, 0)[0])
        column = jnp.where(positions >= index, column / pivot, jnp.zeros_like(column))
        return lax.dynamic_update_slice_in_dim(lower, column[:, None], index, 1)
    return lax.fori_loop(0, order, column_step, jnp.zeros_like(gram_total))

def lower_inverse(lower):
    order = lower.shape[0]
    positions = jnp.arange(order, dtype=jnp.int32)

    def row_step(index, inverse):
        row_of = lax.dynamic_slice_in_dim(lower, index, 1, 0)[0]
        pivot = lax.dynamic_slice_in_dim(row_of, index, 1, 0)[0]
        unit = (positions == index).astype(lower.dtype)
        new_row = (unit - jnp.dot(row_of, inverse, precision=lax.Precision.HIGHEST)) / pivot
        return lax.dynamic_update_slice_in_dim(inverse, new_row[None, :], index, 0)
    return lax.fori_loop(0, order, row_step, jnp.zeros_like(lower))

def apply_factor(y_rounded, gram_total):
    inverse = lower_inverse(lower_cholesky(gram_total))
    solved = jnp.dot(y_rounded.astype(jnp.float32), inverse.T, precision=lax.Precision.HIGHEST)
    return solved.astype(jnp.bfloat16)

def reference(start_panel, block_values, block_rows, block_cols, block_counts):
    nodes_total = GROUP * N_ROW * N_COL
    row_tile = GROUP * N_COL
    col_tile = GROUP * N_ROW
    tiles = jnp.arange(N_ROW * N_COL, dtype=jnp.int32)

    def left_step(carry, tile_id):
        rowidx = (tile_id // N_COL).astype(jnp.int32)
        colidx = (tile_id % N_COL).astype(jnp.int32)
        panel_in = lax.dynamic_slice_in_dim(start_panel, colidx * col_tile, col_tile, 0)
        added = tile_product(block_values[rowidx, colidx], block_rows[rowidx, colidx], block_cols[rowidx, colidx], block_counts[rowidx, colidx], panel_in, BR, False)
        current = lax.dynamic_slice_in_dim(carry, rowidx * row_tile, row_tile, 0)
        return (lax.dynamic_update_slice_in_dim(carry, current + added, rowidx * row_tile, 0), None)
    left_sum, _ = lax.scan(left_step, jnp.zeros((nodes_total, PANEL), jnp.float32), tiles)
    left_y = left_sum.astype(jnp.bfloat16)
    left_gram = jnp.dot(left_y.T, left_y, preferred_element_type=jnp.float32) / nodes_total
    left_panel = apply_factor(left_y, left_gram)

    def right_step(carry, tile_id):
        rowidx = (tile_id // N_COL).astype(jnp.int32)
        colidx = (tile_id % N_COL).astype(jnp.int32)
        panel_in = lax.dynamic_slice_in_dim(left_panel, rowidx * row_tile, row_tile, 0)
        added = tile_product(block_values[rowidx, colidx], block_cols[rowidx, colidx], block_rows[rowidx, colidx], block_counts[rowidx, colidx], panel_in, BC, True)
        current = lax.dynamic_slice_in_dim(carry, colidx * col_tile, col_tile, 0)
        return (lax.dynamic_update_slice_in_dim(carry, current + added, colidx * col_tile, 0), None)
    right_sum, _ = lax.scan(right_step, jnp.zeros((nodes_total, PANEL), jnp.float32), tiles)
    right_y = right_sum.astype(jnp.bfloat16)
    right_gram = jnp.dot(right_y.T, right_y, preferred_element_type=jnp.float32) / nodes_total
    right_panel = apply_factor(right_y, right_gram)
    return (left_panel, right_panel)
```

```python
import functools

import jax
import jax.numpy as jnp
from jax import lax
from jax.experimental import pallas as pl
from jax.experimental.pallas import tpu as pltpu
from jax.sharding import PartitionSpec as P

F32 = jnp.float32
BF16 = jnp.bfloat16
UNROLL = 8
VMEM = pl.BlockSpec(memory_space=pltpu.VMEM)
SMEM = pl.BlockSpec(memory_space=pltpu.SMEM)
ANY = pl.BlockSpec(memory_space=pl.ANY)
HIGH = lax.Precision.HIGHEST


def params():
    return pltpu.CompilerParams(vmem_limit_bytes=60 * 1024 * 1024)


def swap(value, axis, mask):
    size = lax.axis_size(axis)
    return lax.ppermute(value, axis, [(i, i ^ mask) for i in range(size)])


def chunk_of(slots):
    for size in (32, 16, 8):
        if slots % size == 0:
            return size
    return slots


def product_body(axis_size, forward, meta, out_index, in_index, values, shards, panel, vbuf, acc, sems):
    in_me, count = meta[0], meta[2]
    slots = values.shape[0]
    chunk = chunk_of(slots)
    group = min(UNROLL, chunk)
    chunks = slots // chunk
    per_shard = panel.shape[0] // axis_size
    out_blocks = acc.shape[0] - 1

    def panel_copy(k):
        slot = (in_me ^ k) * per_shard
        return pltpu.make_async_copy(shards[k], panel.at[pl.ds(slot, per_shard)], sems.at[chunks + k])

    def value_copy(c):
        span = pl.ds(c * chunk, chunk)
        return pltpu.make_async_copy(values.at[span], vbuf.at[span], sems.at[c])

    for k in range(axis_size):
        panel_copy(k).start()
    for c in range(chunks):
        value_copy(c).start()
    acc[...] = jnp.zeros_like(acc)
    for k in range(axis_size):
        panel_copy(k).wait()

    def one_group(g, carry):
        first = g * group
        products = []
        targets = []
        for u in range(group):
            k = first + u
            block = vbuf[k]
            piece = panel[in_index[k]]
            if forward:
                products.append(jnp.dot(block, piece, preferred_element_type=F32))
            else:
                products.append(jnp.dot(piece, block, preferred_element_type=F32))
            targets.append(jnp.where(k < count, out_index[k], out_blocks))
        for target, product in zip(targets, products):
            acc[target] += product
        return carry

    def one_chunk(c, carry):
        value_copy(c).wait()
        low = c * (chunk // group)
        live = (count + group - 1) // group
        high = jnp.clip(live, low, low + chunk // group)
        return lax.fori_loop(low, high, one_group, carry)

    lax.fori_loop(0, chunks, one_chunk, 0)


def left_kernel(row_size, col_size, meta, rows, cols, values, *refs):
    shards, outs, scratch = refs[:row_size], refs[row_size:-4], refs[-4:]
    panel, vbuf, acc, sems = scratch
    product_body(row_size, True, meta, rows, cols, values, shards, panel, vbuf, acc, sems)
    per = (acc.shape[0] - 1) // col_size
    me = meta[1]
    for k in range(col_size):
        part = acc[pl.ds((me ^ k) * per, per)]
        outs[k][...] = part.astype(outs[k].dtype)


def right_kernel(row_size, col_size, meta, rows, cols, values, *refs):
    shards, (keep, send), scratch = refs[:col_size], refs[col_size:-4], refs[-4:]
    panel, vbuf, acc, sems = scratch
    product_body(col_size, False, meta, cols, rows, values, shards, panel, vbuf, acc, sems)
    per = (acc.shape[0] - 1) // row_size
    me = meta[1]
    for k in range(0, row_size, 2):
        keep[k // 2] = acc[pl.ds((me ^ k) * per, per)]
        send[k // 2] = acc[pl.ds((me ^ (k + 1)) * per, per)].astype(BF16)


def run_product(kernel, meta, rows, cols, values, shards, panel_blocks, out_blocks, out_shape):
    slots, size = values.shape[0], values.shape[-1]
    width = shards[0].shape[-1]
    chunks = slots // chunk_of(slots)
    return pl.pallas_call(
        kernel,
        out_shape=out_shape,
        in_specs=[SMEM, SMEM, SMEM, ANY] + [ANY] * len(shards),
        out_specs=jax.tree.map(lambda _: VMEM, out_shape),
        scratch_shapes=[
            pltpu.VMEM((panel_blocks, size, width), BF16),
            pltpu.VMEM(values.shape, BF16),
            pltpu.VMEM((out_blocks + 1, size, width), F32),
            pltpu.SemaphoreType.DMA((chunks + len(shards),)),
        ],
        compiler_params=params(),
        cost_estimate=pl.CostEstimate(
            flops=2 * slots * size * size * width, bytes_accessed=2 * values.size, transcendentals=0
        ),
    )(meta, rows, cols, values, *shards)


def left_sum_kernel(nodes_total, own, *refs):
    parts, (natural, flipped, gram) = refs[:-3], refs[-3:]
    total = jnp.zeros(gram.shape, F32)
    for b in range(own.shape[0]):
        summed = own[b]
        for part in parts:
            summed = summed + part[b].astype(F32)
        rounded = summed.astype(BF16)
        turned = summed.T.astype(BF16)
        natural[b] = rounded
        flipped[b] = turned
        total = total + jnp.dot(turned, rounded, preferred_element_type=F32)
    gram[...] = total / nodes_total


def core_sum_kernel(keep, came, *outs):
    for k, out in enumerate(outs):
        out[...] = (keep[k] + came[k].astype(F32)).astype(out.dtype)


def right_sum_kernel(nodes_total, inverse, own, *refs):
    parts, (flipped, gram) = refs[:-2], refs[-2:]
    factor = inverse[...]
    total = jnp.zeros(gram.shape, F32)
    for b in range(own.shape[0]):
        summed = own[b]
        for part in parts:
            summed = summed + part[b].astype(F32)
        scaled = jnp.dot(factor, summed, precision=HIGH, preferred_element_type=F32)
        rounded = scaled.astype(BF16)
        flipped[b] = rounded
        total = total + lax.dot_general(rounded, rounded, (((1,), (1,)), ((), ())), preferred_element_type=F32)
    gram[...] = total / nodes_total


def left_apply_kernel(inverse, natural, out):
    factor = inverse[...]
    for b in range(natural.shape[0]):
        solved = lax.dot_general(
            natural[b].astype(F32), factor, (((1,), (1,)), ((), ())), precision=HIGH, preferred_element_type=F32
        )
        out[b] = solved.astype(BF16)


def right_apply_kernel(inverse, flipped, out):
    factor = inverse[...]
    for b in range(flipped.shape[0]):
        solved = jnp.dot(factor, flipped[b].astype(F32), precision=HIGH, preferred_element_type=F32)
        out[b] = solved.T.astype(BF16)


def call(kernel, out_shape, *args):
    return pl.pallas_call(
        kernel,
        out_shape=out_shape,
        in_specs=[VMEM] * len(args),
        out_specs=jax.tree.map(lambda _: VMEM, out_shape),
        compiler_params=params(),
    )(*args)


def shape(dims, kind):
    return jax.ShapeDtypeStruct(dims, kind)


def inverse_factor(gram_total):
    lower = jnp.linalg.cholesky(gram_total)
    identity = jnp.eye(gram_total.shape[0], dtype=F32)
    return jax.scipy.linalg.solve_triangular(lower, identity, lower=True)


def total_gram(gram):
    row_size = lax.axis_size("row")
    col_size = lax.axis_size("col")
    gram = gram + swap(gram, "row", 1)
    came = [swap(gram, "col", k) for k in range(1, col_size)]
    gram = functools.reduce(jnp.add, came, gram)
    came = [swap(gram, "row", k) for k in range(2, row_size, 2)]
    return functools.reduce(jnp.add, came, gram)


def gather_row(shard):
    row_size = lax.axis_size("row")
    have = {0: shard}
    bit = row_size // 2
    while bit:
        for k in sorted(have):
            have[k | bit] = swap(have[k], "row", bit)
        bit //= 2
    return [have[k] for k in range(row_size)]


def local(start_panel, block_values, block_rows, block_cols, block_counts):
    group_rows, width = start_panel.shape
    row_size = lax.axis_size("row")
    col_size = lax.axis_size("col")
    nodes_total = group_rows * row_size * col_size
    values = block_values[0, 0]
    rows, cols = block_rows[0, 0], block_cols[0, 0]
    count = block_counts[0, 0]
    size = values.shape[-1]
    per = group_rows // size
    row_blocks, col_blocks = per * col_size, per * row_size
    row_me = lax.axis_index("row").astype(jnp.int32)
    col_me = lax.axis_index("col").astype(jnp.int32)
    block = (per, size, width)
    square = shape((width, width), F32)

    shards = gather_row(start_panel.reshape(block))
    parts = run_product(
        functools.partial(left_kernel, row_size, col_size),
        jnp.stack([row_me, col_me, count]), rows, cols, values, shards, col_blocks, row_blocks,
        [shape(block, F32)] + [shape(block, BF16)] * (col_size - 1),
    )
    came = [swap(parts[k], "col", k) for k in range(1, col_size)]
    natural, flipped, gram = call(
        functools.partial(left_sum_kernel, nodes_total),
        (shape(block, BF16), shape(block, BF16), square), parts[0], *came,
    )
    turned = [flipped] + [swap(flipped, "col", k) for k in range(1, col_size)]
    inverse = inverse_factor(total_gram(gram))
    left_panel = call(left_apply_kernel, shape(block, BF16), inverse, natural)

    half = (row_size // 2,) + block
    keep, send = run_product(
        functools.partial(right_kernel, row_size, col_size),
        jnp.stack([col_me, row_me, count]), rows, cols, values, turned, row_blocks, col_blocks,
        [shape(half, F32), shape(half, BF16)],
    )
    sums = call(
        core_sum_kernel, [shape(block, F32)] + [shape(block, BF16)] * (row_size // 2 - 1),
        keep, swap(send, "row", 1),
    )
    came = [swap(sums[k // 2], "row", k) for k in range(2, row_size, 2)]
    right_flipped, gram = call(
        functools.partial(right_sum_kernel, nodes_total), (shape(block, BF16), square), inverse, sums[0], *came
    )
    inverse = inverse_factor(total_gram(gram))
    right_panel = call(right_apply_kernel, shape(block, BF16), inverse, right_flipped)
    return (left_panel.reshape(group_rows, width), right_panel.reshape(group_rows, width))


def solution(mesh):
    return jax.shard_map(
        local,
        mesh=mesh,
        in_specs=(
            P(("col", "row"), None),
            P("row", "col", None, None, None),
            P("row", "col", None),
            P("row", "col", None),
            P("row", "col"),
        ),
        out_specs=(P(("row", "col"), None), P(("col", "row"), None)),
        check_vma=False,
    )
```

```python
import functools

import jax
import jax.numpy as jnp
from jax import lax
from jax.experimental import pallas as pl
from jax.experimental.pallas import tpu as pltpu
from jax.sharding import PartitionSpec as P

F32 = jnp.float32
BF16 = jnp.bfloat16
UNROLL = 32
STEP = 8
VMEM = pl.BlockSpec(memory_space=pltpu.VMEM)
SMEM = pl.BlockSpec(memory_space=pltpu.SMEM)
ANY = pl.BlockSpec(memory_space=pl.ANY)
HIGH = lax.Precision.HIGHEST


def params():
    return pltpu.CompilerParams(vmem_limit_bytes=60 * 1024 * 1024)


def swap(value, axis, mask):
    size = lax.axis_size(axis)
    return lax.ppermute(value, axis, [(i, i ^ mask) for i in range(size)])


def chunk_of(slots):
    for size in (32, 16, 8):
        if slots % size == 0:
            return size
    return slots


def product_body(in_axis, forward, counts, out_index, in_index, values, shards, panel, vbuf, acc, sems):
    axis_size = len(shards)
    in_me, count = lax.axis_index(in_axis), counts[0, 0]
    slots = values.shape[2]
    chunk = chunk_of(slots)
    group = min(UNROLL, chunk)
    chunks = slots // chunk
    per_shard = panel.shape[0] // axis_size
    out_blocks = acc.shape[0] - 1

    def panel_copy(k):
        slot = (in_me ^ k) * per_shard
        return pltpu.make_async_copy(shards[k], panel.at[pl.ds(slot, per_shard)], sems.at[chunks + k])

    def value_copy(c):
        span = pl.ds(c * chunk, chunk)
        return pltpu.make_async_copy(values.at[0, 0, span], vbuf.at[span], sems.at[c])

    for k in range(axis_size):
        panel_copy(k).start()
    for c in range(chunks):
        value_copy(c).start()
    acc[...] = jnp.zeros_like(acc)
    for k in range(axis_size):
        panel_copy(k).wait()

    def one_group(g, carry):
        first = g * group
        products = []
        targets = []
        for u in range(group):
            k = first + u
            block = vbuf[k]
            piece = panel[in_index[0, 0, k]]
            if forward:
                products.append(jnp.dot(block, piece, preferred_element_type=F32))
            else:
                products.append(jnp.dot(piece, block, preferred_element_type=F32))
            targets.append(jnp.where(k < count, out_index[0, 0, k], out_blocks))
        for target, product in zip(targets, products):
            acc[target] += product
        return carry

    def one_chunk(c, carry):
        value_copy(c).wait()
        low = c * (chunk // group)
        live = (count + group - 1) // group
        high = jnp.clip(live, low, low + chunk // group)
        return lax.fori_loop(low, high, one_group, carry)

    lax.fori_loop(0, chunks, one_chunk, 0)


def left_kernel(row_size, col_size, counts, rows, cols, values, *refs):
    shards, outs, scratch = refs[:row_size], refs[row_size:-4], refs[-4:]
    panel, vbuf, acc, sems = scratch
    product_body("row", True, counts, rows, cols, values, shards, panel, vbuf, acc, sems)
    per = (acc.shape[0] - 1) // col_size
    me = lax.axis_index("col")
    for k in range(col_size):
        part = acc[pl.ds((me ^ k) * per, per)]
        outs[k][...] = part.astype(outs[k].dtype)


def right_kernel(row_size, col_size, counts, rows, cols, values, *refs):
    shards, (keep, send), scratch = refs[:col_size], refs[col_size:-4], refs[-4:]
    panel, vbuf, acc, sems = scratch
    product_body("col", False, counts, cols, rows, values, shards, panel, vbuf, acc, sems)
    per = (acc.shape[0] - 1) // row_size
    me = lax.axis_index("row")
    for k in range(0, row_size, 2):
        keep[k // 2] = acc[pl.ds((me ^ k) * per, per)]
        send[k // 2] = acc[pl.ds((me ^ (k + 1)) * per, per)].astype(BF16)


def run_product(kernel, counts, rows, cols, values, shards, panel_blocks, out_blocks, out_shape):
    slots, size = values.shape[2], values.shape[-1]
    width = shards[0].shape[-1]
    chunks = slots // chunk_of(slots)
    return pl.pallas_call(
        kernel,
        out_shape=out_shape,
        in_specs=[SMEM, SMEM, SMEM, ANY] + [ANY] * len(shards),
        out_specs=jax.tree.map(lambda _: VMEM, out_shape),
        scratch_shapes=[
            pltpu.VMEM((panel_blocks, size, width), BF16),
            pltpu.VMEM(values.shape[2:], BF16),
            pltpu.VMEM((out_blocks + 1, size, width), F32),
            pltpu.SemaphoreType.DMA((chunks + len(shards),)),
        ],
        compiler_params=params(),
        cost_estimate=pl.CostEstimate(
            flops=2 * slots * size * size * width, bytes_accessed=2 * values.size, transcendentals=0
        ),
    )(counts, rows, cols, values, *shards)


def left_sum_kernel(nodes_total, own, *refs):
    parts, (natural, flipped, gram) = refs[:-3], refs[-3:]
    total = jnp.zeros(gram.shape, F32)
    for b in range(own.shape[0]):
        summed = own[b]
        for part in parts:
            summed = summed + part[b].astype(F32)
        rounded = summed.astype(BF16)
        turned = summed.T.astype(BF16)
        natural[b] = rounded
        flipped[b] = turned
        total = total + jnp.dot(turned, rounded, preferred_element_type=F32)
    gram[...] = total / nodes_total


def core_sum_kernel(keep, came, *outs):
    for k, out in enumerate(outs):
        out[...] = (keep[k] + came[k].astype(F32)).astype(out.dtype)


def inverse_lower(gram):
    order = gram.shape[0]
    panels = order // STEP
    lanes = lax.broadcasted_iota(jnp.int32, (STEP, order), 1)
    strips = [gram[t * STEP:(t + 1) * STEP, :] for t in range(panels)]
    finals = []

    def column(strip, lane):
        return jnp.broadcast_to(strip[:, lane:lane + 1], strip.shape)

    def row(strip, sub):
        return jnp.broadcast_to(strip[sub:sub + 1, :], strip.shape)

    for t in range(panels):
        base = t * STEP
        strip = strips[t]
        cols = [column(strip, base + s) for s in range(STEP)]
        scales, weights, rows_done = [], [], []
        for s in range(STEP):
            scale = lax.rsqrt(row(cols[s], s))
            lower = cols[s] * scale
            scales.append(scale)
            picks = [None] * STEP
            for u in range(s + 1, STEP):
                picks[u] = row(lower, u)
                cols[u] = cols[u] - lower * picks[u]
            weights.append(picks)
            done = jnp.where(lanes == base + s, scale, row(strip, s) * scale)
            done = jnp.where((lanes > base + s) & (lanes < base + STEP), 0.0, done)
            rows_done.append(done)
            if s + 1 < STEP:
                strip = jnp.where(lanes == base + s, 0.0, strip) - lower * done
        sub = lax.broadcasted_iota(jnp.int32, (STEP, order), 0)
        final = rows_done[0]
        for s in range(1, STEP):
            final = jnp.where(sub == s, rows_done[s], final)
        finals.append(jnp.where(lanes <= base + sub, final, 0.0))
        inside = (lanes >= base) & (lanes < base + STEP)
        for v in range(t + 1, panels):
            below = strips[v]
            parts = [column(below, base + s) for s in range(STEP)]
            update = jnp.where(inside, 0.0, below)
            for s in range(STEP):
                part = parts[s] * scales[s]
                for u in range(s + 1, STEP):
                    parts[u] = parts[u] - part * weights[s][u]
                update = update - part * rows_done[s]
            strips[v] = update
    return finals


def limbs(value, depth):
    terms = []
    for _ in range(depth):
        term = value.astype(BF16)
        value = value - term.astype(F32)
        terms.append(term)
    return terms


def fold(stacked, order):
    total = stacked[-order:]
    for low in range(stacked.shape[0] - 2 * order, -1, -order):
        total = stacked[low:low + order] + total
    return total


def factor_of(parts, scratch):
    total = parts[0][...]
    for part in parts[1:]:
        total = total + part[...]
    for t, strip in enumerate(inverse_lower(total)):
        scratch[t * STEP:(t + 1) * STEP, :] = strip
    return scratch[...]


def right_sum_kernel(nodes_total, inverse, own, *refs):
    parts, (flipped, gram) = refs[:-2], refs[-2:]
    order = inverse.shape[0]
    factor = limbs(inverse[...], 3)
    full, head = jnp.concatenate(factor, 0), jnp.concatenate(factor[:2], 0)
    total = jnp.zeros(gram.shape, F32)
    for b in range(own.shape[0]):
        summed = own[b]
        for part in parts:
            summed = summed + part[b].astype(F32)
        first, second = limbs(summed, 2)
        scaled = fold(jnp.dot(head, second, preferred_element_type=F32), order)
        scaled = scaled + fold(jnp.dot(full, first, preferred_element_type=F32), order)
        rounded = scaled.astype(BF16)
        flipped[b] = rounded
        total = total + lax.dot_general(rounded, rounded, (((1,), (1,)), ((), ())), preferred_element_type=F32)
    gram[...] = total / nodes_total


def left_factor_kernel(*refs):
    parts, natural, inverse, out = refs[:-3], refs[-3], refs[-2], refs[-1]
    factor = factor_of(parts, inverse)
    order = factor.shape[0]
    terms = limbs(factor, 3)
    for b in range(natural.shape[0]):
        solved = jnp.zeros(out.shape[1:], F32)
        for term in reversed(terms):
            solved = solved + lax.dot_general(
                natural[b], term, (((1,), (1,)), ((), ())), preferred_element_type=F32
            )
        out[b] = solved.astype(BF16)


def right_factor_kernel(*refs):
    parts, flipped, out, scratch = refs[:-3], refs[-3], refs[-2], refs[-1]
    factor = factor_of(parts, scratch)
    stacked = jnp.concatenate(limbs(factor, 3), 0)
    for b in range(flipped.shape[0]):
        solved = fold(jnp.dot(stacked, flipped[b], preferred_element_type=F32), factor.shape[0])
        out[b] = solved.T.astype(BF16)


def call(kernel, out_shape, *args, scratch=()):
    return pl.pallas_call(
        kernel,
        out_shape=out_shape,
        in_specs=[VMEM] * len(args),
        out_specs=jax.tree.map(lambda _: VMEM, out_shape),
        scratch_shapes=scratch,
        compiler_params=params(),
    )(*args)


def shape(dims, kind):
    return jax.ShapeDtypeStruct(dims, kind)


def exchange(value, axis, first, step=1):
    return [value] + [swap(value, axis, k) for k in range(first, lax.axis_size(axis), step)]


def gather_row(shard):
    row_size = lax.axis_size("row")
    have = {0: shard}
    bit = row_size // 2
    while bit:
        for k in sorted(have):
            have[k | bit] = swap(have[k], "row", bit)
        bit //= 2
    return [have[k] for k in range(row_size)]


def local(start_panel, block_values, block_rows, block_cols, block_counts):
    group_rows, width = start_panel.shape
    row_size = lax.axis_size("row")
    col_size = lax.axis_size("col")
    nodes_total = group_rows * row_size * col_size
    size = block_values.shape[-1]
    lists = (block_counts, block_rows, block_cols, block_values)
    per = group_rows // size
    row_blocks, col_blocks = per * col_size, per * row_size
    block = (per, size, width)
    square = shape((width, width), F32)

    shards = gather_row(start_panel.reshape(block))
    parts = run_product(
        functools.partial(left_kernel, row_size, col_size),
        *lists, shards, col_blocks, row_blocks,
        [shape(block, F32)] + [shape(block, BF16)] * (col_size - 1),
    )
    came = [swap(parts[k], "col", k) for k in range(1, col_size)]
    natural, flipped, gram = call(
        functools.partial(left_sum_kernel, nodes_total),
        (shape(block, BF16), shape(block, BF16), square), parts[0], *came,
    )
    turned = exchange(flipped, "col", 1)
    gram = gram + swap(gram, "row", 1)
    gram = functools.reduce(jnp.add, exchange(gram, "row", 2, 2))

    half = (row_size // 2,) + block
    keep, send = run_product(
        functools.partial(right_kernel, row_size, col_size),
        *lists, turned, row_blocks, col_blocks,
        [shape(half, F32), shape(half, BF16)],
    )
    sums = call(
        core_sum_kernel, [shape(block, F32)] + [shape(block, BF16)] * (row_size // 2 - 1),
        keep, swap(send, "row", 1),
    )
    came = [swap(sums[k // 2], "row", k) for k in range(2, row_size, 2)]
    gram, _ = lax.optimization_barrier((gram, sums[-1]))
    inverse, left_panel = call(
        left_factor_kernel, (square, shape(block, BF16)), *exchange(gram, "col", 1), natural
    )
    right_flipped, gram = call(
        functools.partial(right_sum_kernel, nodes_total), (shape(block, BF16), square), inverse, sums[0], *came
    )
    gram = gram + swap(gram, "row", 1)
    gram = functools.reduce(jnp.add, exchange(gram, "col", 1))
    right_panel = call(
        right_factor_kernel, shape(block, BF16), *exchange(gram, "row", 2, 2), right_flipped,
        scratch=[pltpu.VMEM((width, width), F32)],
    )
    return (left_panel.reshape(group_rows, width), right_panel.reshape(group_rows, width))


def solution(mesh):
    return jax.shard_map(
        local,
        mesh=mesh,
        in_specs=(
            P(("col", "row"), None),
            P("row", "col", None, None, None),
            P("row", "col", None),
            P("row", "col", None),
            P("row", "col"),
        ),
        out_specs=(P(("row", "col"), None), P(("col", "row"), None)),
        check_vma=False,
    )
```

```python
import functools

import jax
import jax.numpy as jnp
from jax import lax
from jax.experimental import pallas as pl
from jax.experimental.pallas import tpu as pltpu
from jax.sharding import PartitionSpec as P


F32 = jnp.float32
BF16 = jnp.bfloat16
UNROLL = 32
STEP = 8
MARGIN = 4 * 1024 * 1024
VMEM = pl.BlockSpec(memory_space=pltpu.VMEM)
SMEM = pl.BlockSpec(memory_space=pltpu.SMEM)
ANY = pl.BlockSpec(memory_space=pl.ANY)
HBM = pl.BlockSpec(memory_space=pltpu.HBM)


def nbytes(item):
    total = jnp.dtype(item.dtype).itemsize
    for extent in item.shape:
        total *= extent
    return total


def params(items):
    return pltpu.CompilerParams(vmem_limit_bytes=sum(map(nbytes, items)) + MARGIN)


def swap(value, axis, mask):
    size = lax.axis_size(axis)
    return lax.ppermute(value, axis, [(i, i ^ mask) for i in range(size)])


def group_of(slots):
    return max(size for size in range(1, UNROLL + 1) if slots % size == 0)


def product_body(in_axis, forward, counts, lists, values, shards, scratch):
    in_me, count = lax.axis_index(in_axis), counts[0, 0]
    panel, acc, index, sems = scratch
    per_shard = panel.shape[0] // len(shards)
    out_blocks = acc.shape[0] - 1
    group = group_of(values.shape[0])
    out_row, in_row = (0, 1) if forward else (1, 0)
    copies = [pltpu.make_async_copy(lists, index, sems.at[0])]
    for k, shard in enumerate(shards):
        place = panel.at[pl.ds((in_me ^ k) * per_shard, per_shard)]
        copies.append(pltpu.make_async_copy(shard, place, sems.at[k + 1]))
    for copy in copies:
        copy.start()
    acc[...] = jnp.zeros_like(acc)
    for copy in copies:
        copy.wait()

    def one_group(g, carry):
        first = g * group
        products = []
        targets = []
        for u in range(group):
            k = first + u
            block = values[k]
            piece = panel[index[in_row, k]]
            if forward:
                products.append(jnp.dot(block, piece, preferred_element_type=F32))
            else:
                products.append(jnp.dot(piece, block, preferred_element_type=F32))
            targets.append(jnp.where(k < count, index[out_row, k], out_blocks))
        for target, product in zip(targets, products):
            acc[target] += product
        return carry

    lax.fori_loop(0, (count + group - 1) // group, one_group, 0)


def left_kernel(row_size, col_size, counts, lists, values, *refs):
    shards, outs, scratch = refs[:row_size], refs[row_size:-4], refs[-4:]
    acc = scratch[1]
    product_body("row", True, counts, lists, values, shards, scratch)
    per = (acc.shape[0] - 1) // col_size
    me = lax.axis_index("col")
    for k in range(col_size):
        part = acc[pl.ds((me ^ k) * per, per)]
        outs[k][...] = part.astype(outs[k].dtype)


def right_kernel(row_size, col_size, counts, lists, values, *refs):
    shards, (keep, send), scratch = refs[:col_size], refs[col_size:-4], refs[-4:]
    acc = scratch[1]
    product_body("col", False, counts, lists, values, shards, scratch)
    per = (acc.shape[0] - 1) // row_size
    me = lax.axis_index("row")
    for k in range(0, row_size, 2):
        keep[k // 2] = acc[pl.ds((me ^ k) * per, per)]
        send[k // 2] = acc[pl.ds((me ^ (k + 1)) * per, per)].astype(BF16)


def run_product(kernel, first, counts, lists, values, shards, panel_blocks, out_blocks, out_shape):
    slots, size = values.shape[0], values.shape[-1]
    width = shards[0].shape[-1]
    held = [
        pltpu.VMEM((panel_blocks, size, width), BF16),
        pltpu.VMEM((out_blocks + 1, size, width), F32),
    ]
    return pl.pallas_call(
        kernel,
        out_shape=out_shape,
        in_specs=[SMEM, ANY, VMEM, first] + [ANY] * (len(shards) - 1),
        out_specs=jax.tree.map(lambda _: VMEM, out_shape),
        scratch_shapes=held
        + [pltpu.SMEM(lists.shape, jnp.int32), pltpu.SemaphoreType.DMA((len(shards) + 1,))],
        compiler_params=params(held + list(out_shape) + [values]),
        cost_estimate=pl.CostEstimate(
            flops=2 * slots * size * size * width, bytes_accessed=2 * values.size, transcendentals=0
        ),
    )(counts, lists, values, *shards)


def stage_kernel(rows, cols, values, lists, staged, sem):
    copy = pltpu.make_async_copy(values.at[0, 0], staged, sem)
    copy.start()
    lists[0], lists[1] = rows[0, 0], cols[0, 0]
    copy.wait()


def left_sum_kernel(nodes_total, own, *refs):
    parts, (natural, flipped, gram) = refs[:-3], refs[-3:]
    total = jnp.zeros(gram.shape, F32)
    for b in range(own.shape[0]):
        summed = own[b]
        for part in parts:
            summed = summed + part[b].astype(F32)
        rounded = summed.astype(BF16)
        turned = summed.T.astype(BF16)
        natural[b] = rounded
        flipped[b] = turned
        total = total + jnp.dot(turned, rounded, preferred_element_type=F32)
    gram[...] = total / nodes_total


def core_sum_kernel(keep, came, *outs):
    for k, out in enumerate(outs):
        out[...] = (keep[k] + came[k].astype(F32)).astype(out.dtype)


def inverse_lower(gram):
    order = gram.shape[0]
    panels = order // STEP
    lanes = lax.broadcasted_iota(jnp.int32, (STEP, order), 1)
    strips = [gram[t * STEP:(t + 1) * STEP, :] for t in range(panels)]
    finals = []

    def column(strip, lane):
        return jnp.broadcast_to(strip[:, lane:lane + 1], strip.shape)

    def row(strip, sub):
        return jnp.broadcast_to(strip[sub:sub + 1, :], strip.shape)

    for t in range(panels):
        base = t * STEP
        strip = strips[t]
        cols = [column(strip, base + s) for s in range(STEP)]
        scales, weights, rows_done = [], [], []
        for s in range(STEP):
            scale = lax.rsqrt(row(cols[s], s))
            lower = cols[s] * scale
            scales.append(scale)
            picks = [None] * STEP
            for u in range(s + 1, STEP):
                picks[u] = row(lower, u)
                cols[u] = cols[u] - lower * picks[u]
            weights.append(picks)
            done = jnp.where(lanes == base + s, scale, row(strip, s) * scale)
            done = jnp.where((lanes > base + s) & (lanes < base + STEP), 0.0, done)
            rows_done.append(done)
            if s + 1 < STEP:
                strip = jnp.where(lanes == base + s, 0.0, strip) - lower * done
        sub = lax.broadcasted_iota(jnp.int32, (STEP, order), 0)
        final = rows_done[0]
        for s in range(1, STEP):
            final = jnp.where(sub == s, rows_done[s], final)
        finals.append(jnp.where(lanes <= base + sub, final, 0.0))
        inside = (lanes >= base) & (lanes < base + STEP)
        for v in range(t + 1, panels):
            below = strips[v]
            parts = [column(below, base + s) for s in range(STEP)]
            update = jnp.where(inside, 0.0, below)
            for s in range(STEP):
                part = parts[s] * scales[s]
                for u in range(s + 1, STEP):
                    parts[u] = parts[u] - part * weights[s][u]
                update = update - part * rows_done[s]
            strips[v] = update
    return finals


def limbs(value, depth):
    terms = []
    for _ in range(depth):
        term = value.astype(BF16)
        value = value - term.astype(F32)
        terms.append(term)
    return terms


def fold(stacked, order):
    total = stacked[-order:]
    for low in range(stacked.shape[0] - 2 * order, -1, -order):
        total = stacked[low:low + order] + total
    return total


def factor_of(parts, scratch):
    total = parts[0][...]
    for part in parts[1:]:
        total = total + part[...].astype(F32)
    for t, strip in enumerate(inverse_lower(total)):
        scratch[t * STEP:(t + 1) * STEP, :] = strip
    return scratch[...]


def right_sum_kernel(nodes_total, inverse, own, *refs):
    parts, (flipped, gram) = refs[:-2], refs[-2:]
    order = inverse.shape[0]
    factor = limbs(inverse[...], 3)
    full, head = jnp.concatenate(factor, 0), jnp.concatenate(factor[:2], 0)
    total = jnp.zeros(gram.shape, F32)
    for b in range(own.shape[0]):
        summed = own[b]
        for part in parts:
            summed = summed + part[b].astype(F32)
        first, second = limbs(summed, 2)
        scaled = fold(jnp.dot(head, second, preferred_element_type=F32), order)
        scaled = scaled + fold(jnp.dot(full, first, preferred_element_type=F32), order)
        rounded = scaled.astype(BF16)
        flipped[b] = rounded
        total = total + lax.dot_general(rounded, rounded, (((1,), (1,)), ((), ())), preferred_element_type=F32)
    gram[...] = total / nodes_total


def left_factor_kernel(*refs):
    parts, natural, inverse, out = refs[:-3], refs[-3], refs[-2], refs[-1]
    factor = factor_of(parts, inverse)
    terms = limbs(factor, 3)
    for b in range(natural.shape[0]):
        solved = jnp.zeros(out.shape[1:], F32)
        for term in reversed(terms):
            solved = solved + lax.dot_general(
                natural[b], term, (((1,), (1,)), ((), ())), preferred_element_type=F32
            )
        out[b] = solved.astype(BF16)


def right_factor_kernel(*refs):
    parts, flipped, out, scratch = refs[:-3], refs[-3], refs[-2], refs[-1]
    factor = factor_of(parts, scratch)
    stacked = jnp.concatenate(limbs(factor, 3), 0)
    for b in range(flipped.shape[0]):
        solved = fold(jnp.dot(stacked, flipped[b], preferred_element_type=F32), factor.shape[0])
        out[b] = solved.T.astype(BF16)


def call(kernel, out_shape, *args, scratch=()):
    return pl.pallas_call(
        kernel,
        out_shape=out_shape,
        in_specs=[VMEM] * len(args),
        out_specs=jax.tree.map(lambda _: VMEM, out_shape),
        scratch_shapes=scratch,
        compiler_params=params(list(args) + jax.tree.leaves(out_shape) + list(scratch)),
    )(*args)


def shape(dims, kind):
    return jax.ShapeDtypeStruct(dims, kind)


def exchange(value, axis, first, step=1):
    sent = value.astype(BF16)
    return [value] + [swap(sent, axis, k) for k in range(first, lax.axis_size(axis), step)]


def add_parts(parts):
    return functools.reduce(lambda total, part: total + part.astype(total.dtype), parts)


def gather_row(shard):
    row_size = lax.axis_size("row")
    have = {0: shard}
    bit = row_size // 2
    while bit:
        for k in sorted(have):
            have[k | bit] = swap(have[k], "row", bit)
        bit //= 2
    return [have[k] for k in range(row_size)]


def local(start_panel, block_values, block_rows, block_cols, block_counts):
    group_rows, width = start_panel.shape
    row_size = lax.axis_size("row")
    col_size = lax.axis_size("col")
    nodes_total = group_rows * row_size * col_size
    size = block_values.shape[-1]
    slots = block_values.shape[2]
    staged = (shape((2, slots), jnp.int32), shape((slots, size, size), BF16))
    lists, values = pl.pallas_call(
        stage_kernel,
        out_shape=staged,
        in_specs=[VMEM, VMEM, HBM],
        out_specs=(VMEM, VMEM),
        scratch_shapes=[pltpu.SemaphoreType.DMA(())],
        compiler_params=params(staged),
    )(block_rows, block_cols, block_values)
    tile = (block_counts, lists, values)
    per = group_rows // size
    row_blocks, col_blocks = per * col_size, per * row_size
    block = (per, size, width)
    square = shape((width, width), F32)

    shards = gather_row(start_panel.reshape(block))
    parts = run_product(
        functools.partial(left_kernel, row_size, col_size), HBM,
        *tile, shards, col_blocks, row_blocks,
        [shape(block, F32)] + [shape(block, BF16)] * (col_size - 1),
    )
    came = [swap(parts[k], "col", k) for k in range(1, col_size)]
    natural, flipped, gram = call(
        functools.partial(left_sum_kernel, nodes_total),
        (shape(block, BF16), shape(block, BF16), square), parts[0], *came,
    )
    turned = exchange(flipped, "col", 1)
    gram = add_parts(exchange(gram + swap(gram, "row", 1), "row", 2, 2))
    gram, turned = lax.optimization_barrier((gram, turned))

    half = (row_size // 2,) + block
    keep, send = run_product(
        functools.partial(right_kernel, row_size, col_size), ANY,
        *tile, turned, row_blocks, col_blocks,
        [shape(half, F32), shape(half, BF16)],
    )
    sums = call(
        core_sum_kernel, [shape(block, F32)] + [shape(block, BF16)] * (row_size // 2 - 1),
        keep, swap(send, "row", 1),
    )
    came = [swap(sums[k // 2], "row", k) for k in range(2, row_size, 2)]
    gram, _ = lax.optimization_barrier((gram, sums[-1]))
    grams = exchange(gram, "col", 1)
    inverse, left_panel = call(left_factor_kernel, (square, shape(block, BF16)), *grams, natural)
    right_flipped, gram = call(
        functools.partial(right_sum_kernel, nodes_total), (shape(block, BF16), square), inverse, sums[0], *came
    )
    gram = gram + swap(gram, "row", 1)
    gram = add_parts(exchange(gram, "col", 1))
    right_panel = call(
        right_factor_kernel, shape(block, BF16), *exchange(gram, "row", 2, 2), right_flipped,
        scratch=[pltpu.VMEM((width, width), F32)],
    )
    return (left_panel.reshape(group_rows, width), right_panel.reshape(group_rows, width))


def solution(mesh):
    return jax.shard_map(
        local,
        mesh=mesh,
        in_specs=(
            P(("col", "row"), None),
            P("row", "col", None, None, None),
            P("row", "col", None),
            P("row", "col", None),
            P("row", "col"),
        ),
        out_specs=(P(("row", "col"), None), P(("col", "row"), None)),
        check_vma=False,
    )
```

```python
import functools

import jax
import jax.numpy as jnp
from jax import lax
from jax.experimental import pallas as pl
from jax.experimental.pallas import tpu as pltpu
from jax.sharding import PartitionSpec as P


F32 = jnp.float32
BF16 = jnp.bfloat16
UNROLL = 32
STEP = 8
MARGIN = 4 * 1024 * 1024
VMEM = pl.BlockSpec(memory_space=pltpu.VMEM)
SMEM = pl.BlockSpec(memory_space=pltpu.SMEM)
ANY = pl.BlockSpec(memory_space=pl.ANY)
HBM = pl.BlockSpec(memory_space=pltpu.HBM)


def nbytes(item):
    total = jnp.dtype(item.dtype).itemsize
    for extent in item.shape:
        total *= extent
    return total


def params(items):
    return pltpu.CompilerParams(vmem_limit_bytes=sum(map(nbytes, items)) + MARGIN)


def swap(value, axis, mask):
    size = lax.axis_size(axis)
    return lax.ppermute(value, axis, [(i, i ^ mask) for i in range(size)])


def group_of(slots):
    return max(size for size in range(1, UNROLL + 1) if slots % size == 0)


def product_body(in_axis, forward, counts, lists, values, shards, scratch):
    in_me, count = lax.axis_index(in_axis), counts[0, 0]
    panel, acc, index, sems = scratch
    out_blocks = acc.shape[0] - 1
    group = group_of(values.shape[0])
    out_row, in_row = (0, 1) if forward else (1, 0)
    copies = [pltpu.make_async_copy(lists, index, sems.at[0])]
    for k, pieces in enumerate(shards):
        length = sum(piece.shape[0] for piece in pieces)
        first = (in_me ^ k) * length
        for piece in pieces:
            place = panel.at[pl.ds(first, piece.shape[0])]
            copies.append(pltpu.make_async_copy(piece, place, sems.at[len(copies)]))
            first = first + piece.shape[0]
    for copy in copies:
        copy.start()
    acc[...] = jnp.zeros_like(acc)
    for copy in copies:
        copy.wait()

    def one_group(g, carry):
        first = g * group
        products = []
        targets = []
        for u in range(group):
            k = first + u
            block = values[k]
            piece = panel[index[in_row, k]]
            if forward:
                products.append(jnp.dot(block, piece, preferred_element_type=F32))
            else:
                products.append(jnp.dot(piece, block, preferred_element_type=F32))
            targets.append(jnp.where(k < count, index[out_row, k], out_blocks))
        for target, product in zip(targets, products):
            acc[target] += product
        return carry

    lax.fori_loop(0, (count + group - 1) // group, one_group, 0)


def nested(form, refs):
    refs = iter(refs)
    return [[next(refs) for _ in range(pieces)] for pieces in form]


def halves(value):
    middle = value.shape[0] // 2
    return [value[:middle], value[middle:]] if middle else [value]


def block_of(pieces, b):
    for piece in pieces:
        if b < piece.shape[0]:
            return piece[b].astype(F32)
        b -= piece.shape[0]


def left_kernel(form, col_size, counts, lists, values, *refs):
    shards, outs, scratch = nested(form, refs), refs[sum(form):-4], refs[-4:]
    acc = scratch[1]
    product_body("row", True, counts, lists, values, shards, scratch)
    per = (acc.shape[0] - 1) // col_size
    me = lax.axis_index("col")
    for k in range(col_size):
        part = acc[pl.ds((me ^ k) * per, per)]
        outs[k][...] = part.astype(outs[k].dtype)


def right_kernel(form, row_size, counts, lists, values, *refs):
    shards, (keep, send), scratch = nested(form, refs), refs[sum(form):-4], refs[-4:]
    acc = scratch[1]
    product_body("col", False, counts, lists, values, shards, scratch)
    per = (acc.shape[0] - 1) // row_size
    me = lax.axis_index("row")
    for k in range(0, row_size, 2):
        keep[k // 2] = acc[pl.ds((me ^ k) * per, per)]
        send[k // 2] = acc[pl.ds((me ^ (k + 1)) * per, per)].astype(BF16)


def run_product(kernel, other, first, counts, lists, values, shards, panel_blocks, out_blocks, out_shape):
    slots, size = values.shape[0], values.shape[-1]
    width = shards[0][0].shape[-1]
    form = tuple(map(len, shards))
    shards = jax.tree.leaves(shards)
    held = [
        pltpu.VMEM((panel_blocks, size, width), BF16),
        pltpu.VMEM((out_blocks + 1, size, width), F32),
    ]
    return pl.pallas_call(
        functools.partial(kernel, form, other),
        out_shape=out_shape,
        in_specs=[SMEM, ANY, VMEM, first] + [ANY] * (len(shards) - 1),
        out_specs=jax.tree.map(lambda _: VMEM, out_shape),
        scratch_shapes=held
        + [pltpu.SMEM(lists.shape, jnp.int32), pltpu.SemaphoreType.DMA((len(shards) + 1,))],
        compiler_params=params(held + list(out_shape) + [values]),
        cost_estimate=pl.CostEstimate(
            flops=2 * slots * size * size * width, bytes_accessed=2 * values.size, transcendentals=0
        ),
    )(counts, lists, values, *shards)


def stage_kernel(rows, cols, values, lists, staged, sem):
    copy = pltpu.make_async_copy(values.at[0, 0], staged, sem)
    copy.start()
    lists[0], lists[1] = rows[0, 0], cols[0, 0]
    copy.wait()


def left_sum_kernel(nodes_total, own, *refs):
    parts, (natural, flipped, gram) = refs[:-3], refs[-3:]
    total = jnp.zeros(gram.shape, F32)
    for b in range(own.shape[0]):
        summed = own[b]
        for part in parts:
            summed = summed + part[b].astype(F32)
        rounded = summed.astype(BF16)
        turned = summed.T.astype(BF16)
        natural[b] = rounded
        flipped[b] = turned
        total = total + jnp.dot(turned, rounded, preferred_element_type=F32)
    gram[...] = total / nodes_total


def core_sum_kernel(form, keep, came, *outs):
    for k, pieces in enumerate(nested(form, outs)):
        first = 0
        for out in pieces:
            span = pl.ds(first, out.shape[0])
            out[...] = (keep[k, span] + came[k, span].astype(F32)).astype(out.dtype)
            first += out.shape[0]


def inverse_lower(gram):
    order = gram.shape[0]
    panels = order // STEP
    lanes = lax.broadcasted_iota(jnp.int32, (STEP, order), 1)
    strips = [gram[t * STEP:(t + 1) * STEP, :] for t in range(panels)]
    finals = []

    def column(strip, lane):
        return jnp.broadcast_to(strip[:, lane:lane + 1], strip.shape)

    def row(strip, sub):
        return jnp.broadcast_to(strip[sub:sub + 1, :], strip.shape)

    for t in range(panels):
        base = t * STEP
        strip = strips[t]
        cols = [column(strip, base + s) for s in range(STEP)]
        scales, weights, rows_done = [], [], []
        for s in range(STEP):
            scale = lax.rsqrt(row(cols[s], s))
            lower = cols[s] * scale
            scales.append(scale)
            picks = [None] * STEP
            for u in range(s + 1, STEP):
                picks[u] = row(lower, u)
                cols[u] = cols[u] - lower * picks[u]
            weights.append(picks)
            done = jnp.where(lanes == base + s, scale, row(strip, s) * scale)
            done = jnp.where((lanes > base + s) & (lanes < base + STEP), 0.0, done)
            rows_done.append(done)
            if s + 1 < STEP:
                strip = jnp.where(lanes == base + s, 0.0, strip) - lower * done
        sub = lax.broadcasted_iota(jnp.int32, (STEP, order), 0)
        final = rows_done[0]
        for s in range(1, STEP):
            final = jnp.where(sub == s, rows_done[s], final)
        finals.append(jnp.where(lanes <= base + sub, final, 0.0))
        inside = (lanes >= base) & (lanes < base + STEP)
        for v in range(t + 1, panels):
            below = strips[v]
            parts = [column(below, base + s) for s in range(STEP)]
            update = jnp.where(inside, 0.0, below)
            for s in range(STEP):
                part = parts[s] * scales[s]
                for u in range(s + 1, STEP):
                    parts[u] = parts[u] - part * weights[s][u]
                update = update - part * rows_done[s]
            strips[v] = update
    return finals


def limbs(value, depth):
    terms = []
    for _ in range(depth):
        term = value.astype(BF16)
        value = value - term.astype(F32)
        terms.append(term)
    return terms


def fold(stacked, order):
    total = stacked[-order:]
    for low in range(stacked.shape[0] - 2 * order, -1, -order):
        total = stacked[low:low + order] + total
    return total


def factor_of(parts, scratch):
    total = parts[0][...]
    for part in parts[1:]:
        total = total + part[...].astype(F32)
    for t, strip in enumerate(inverse_lower(total)):
        scratch[t * STEP:(t + 1) * STEP, :] = strip
    return scratch[...]


def right_sum_kernel(form, nodes_total, inverse, own, *refs):
    parts, (flipped, gram) = nested(form, refs), refs[-2:]
    order = inverse.shape[0]
    factor = limbs(inverse[...], 3)
    full, head = jnp.concatenate(factor, 0), jnp.concatenate(factor[:2], 0)
    total = jnp.zeros(gram.shape, F32)
    for b in range(own.shape[0]):
        summed = own[b]
        for part in parts:
            summed = summed + block_of(part, b)
        first, second = limbs(summed, 2)
        scaled = fold(jnp.dot(head, second, preferred_element_type=F32), order)
        scaled = scaled + fold(jnp.dot(full, first, preferred_element_type=F32), order)
        rounded = scaled.astype(BF16)
        flipped[b] = rounded
        total = total + lax.dot_general(rounded, rounded, (((1,), (1,)), ((), ())), preferred_element_type=F32)
    gram[...] = total / nodes_total


def left_factor_kernel(*refs):
    parts, natural, inverse, out = refs[:-3], refs[-3], refs[-2], refs[-1]
    factor = factor_of(parts, inverse)
    terms = limbs(factor, 3)
    for b in range(natural.shape[0]):
        solved = jnp.zeros(out.shape[1:], F32)
        for term in reversed(terms):
            solved = solved + lax.dot_general(
                natural[b], term, (((1,), (1,)), ((), ())), preferred_element_type=F32
            )
        out[b] = solved.astype(BF16)


def right_factor_kernel(*refs):
    parts, flipped, out, scratch = refs[:-3], refs[-3], refs[-2], refs[-1]
    factor = factor_of(parts, scratch)
    stacked = jnp.concatenate(limbs(factor, 3), 0)
    for b in range(flipped.shape[0]):
        solved = fold(jnp.dot(stacked, flipped[b], preferred_element_type=F32), factor.shape[0])
        out[b] = solved.T.astype(BF16)


def call(kernel, out_shape, *args, scratch=()):
    return pl.pallas_call(
        kernel,
        out_shape=out_shape,
        in_specs=[VMEM] * len(args),
        out_specs=jax.tree.map(lambda _: VMEM, out_shape),
        scratch_shapes=scratch,
        compiler_params=params(list(args) + jax.tree.leaves(out_shape) + list(scratch)),
    )(*args)


def shape(dims, kind):
    return jax.ShapeDtypeStruct(dims, kind)


def exchange(value, axis, first, step=1):
    sent = value.astype(BF16)
    return [value] + [swap(sent, axis, k) for k in range(first, lax.axis_size(axis), step)]


def add_parts(parts):
    return functools.reduce(lambda total, part: total + part.astype(total.dtype), parts)


def gather_row(shard):
    row_size = lax.axis_size("row")
    top = row_size // 2
    have = {0: [shard], top: [swap(piece, "row", top) for piece in halves(shard)]}
    bit = top // 2
    while bit:
        for k in sorted(have, reverse=True):
            have[k | bit] = [swap(piece, "row", bit) for piece in have[k]]
        bit //= 2
    return [have[k] for k in range(row_size)]


def collect_row(terms):
    row_size = lax.axis_size("row")
    came = []
    bit = 2
    while bit < row_size:
        for k in sorted(terms, reverse=True):
            if not k & bit:
                continue
            moved = [swap(piece.astype(BF16), "row", bit) for piece in terms.pop(k)]
            if k ^ bit:
                terms[k ^ bit] = [(a + b.astype(F32)) for a, b in zip(terms[k ^ bit], moved)]
            else:
                came.append(moved)
        bit *= 2
    return came


def local(start_panel, block_values, block_rows, block_cols, block_counts):
    group_rows, width = start_panel.shape
    row_size = lax.axis_size("row")
    col_size = lax.axis_size("col")
    nodes_total = group_rows * row_size * col_size
    size = block_values.shape[-1]
    slots = block_values.shape[2]
    staged = (shape((2, slots), jnp.int32), shape((slots, size, size), BF16))
    lists, values = pl.pallas_call(
        stage_kernel,
        out_shape=staged,
        in_specs=[VMEM, VMEM, HBM],
        out_specs=(VMEM, VMEM),
        scratch_shapes=[pltpu.SemaphoreType.DMA(())],
        compiler_params=params(staged),
    )(block_rows, block_cols, block_values)
    tile = (block_counts, lists, values)
    per = group_rows // size
    row_blocks, col_blocks = per * col_size, per * row_size
    block = (per, size, width)
    square = shape((width, width), F32)

    shards = gather_row(start_panel.reshape(block))
    parts = run_product(
        left_kernel, col_size, HBM,
        *tile, shards, col_blocks, row_blocks,
        [shape(block, F32)] + [shape(block, BF16)] * (col_size - 1),
    )
    came = [swap(parts[k], "col", k) for k in range(1, col_size)]
    natural, flipped, gram = call(
        functools.partial(left_sum_kernel, nodes_total),
        (shape(block, BF16), shape(block, BF16), square), parts[0], *came,
    )
    turned = exchange(flipped, "col", 1)
    gram = add_parts(exchange(gram + swap(gram, "row", 1), "row", 2, 2))
    gram, turned = lax.optimization_barrier((gram, turned))

    half = (row_size // 2,) + block
    keep, send = run_product(
        right_kernel, row_size, ANY,
        *tile, [[part] for part in turned], row_blocks, col_blocks,
        [shape(half, F32), shape(half, BF16)],
    )
    pieces = {0: [shape(block, F32)]}
    for k in range(2, row_size, 2):
        far = 2 if k & (row_size // 2) and per % 2 == 0 else 1
        kind = BF16 if k & 2 else F32
        pieces[k] = [shape((per // far, size, width), kind)] * far
    form = tuple(map(len, pieces.values()))
    sums = call(
        functools.partial(core_sum_kernel, form), jax.tree.leaves(list(pieces.values())), keep, swap(send, "row", 1)
    )
    terms = dict(zip(pieces, nested(form, sums)))
    (own,) = terms.pop(0)
    gram, _ = lax.optimization_barrier((gram, own))
    came = collect_row(terms)
    grams = exchange(gram, "col", 1)
    inverse, left_panel = call(left_factor_kernel, (square, shape(block, BF16)), *grams, natural)
    right_flipped, gram = call(
        functools.partial(right_sum_kernel, tuple(map(len, came)), nodes_total),
        (shape(block, BF16), square), inverse, own, *jax.tree.leaves(came),
    )
    gram = gram + swap(gram, "row", 1)
    gram = add_parts(exchange(gram, "col", 1))
    right_panel = call(
        right_factor_kernel, shape(block, BF16), *exchange(gram, "row", 2, 2), right_flipped,
        scratch=[pltpu.VMEM((width, width), F32)],
    )
    return (left_panel.reshape(group_rows, width), right_panel.reshape(group_rows, width))


def solution(mesh):
    return jax.shard_map(
        local,
        mesh=mesh,
        in_specs=(
            P(("col", "row"), None),
            P("row", "col", None, None, None),
            P("row", "col", None),
            P("row", "col", None),
            P("row", "col"),
        ),
        out_specs=(P(("row", "col"), None), P(("col", "row"), None)),
        check_vma=False,
    )
```

```python
import functools

import jax
import jax.numpy as jnp
from jax import lax
from jax.experimental import pallas as pl
from jax.experimental.pallas import tpu as pltpu
from jax.sharding import PartitionSpec as P


F32 = jnp.float32
BF16 = jnp.bfloat16
UNROLL = 32
STEP = 8
MARGIN = 4 * 1024 * 1024
VMEM = pl.BlockSpec(memory_space=pltpu.VMEM)
SMEM = pl.BlockSpec(memory_space=pltpu.SMEM)
ANY = pl.BlockSpec(memory_space=pl.ANY)
HBM = pl.BlockSpec(memory_space=pltpu.HBM)


def nbytes(item):
    total = jnp.dtype(item.dtype).itemsize
    for extent in item.shape:
        total *= extent
    return total


def params(items):
    return pltpu.CompilerParams(vmem_limit_bytes=sum(map(nbytes, items)) + MARGIN)


def swap(value, axis, mask):
    size = lax.axis_size(axis)
    return lax.ppermute(value, axis, [(i, i ^ mask) for i in range(size)])


def product_body(in_axis, forward, second, lists, values, shards, scratch, carried=None):
    in_me = lax.axis_index(in_axis)
    panel, acc, index, sems = scratch
    copies = [pltpu.make_async_copy(lists, index, sems.at[0])]
    for k, pieces in shards:
        length = sum(piece.shape[0] for piece in pieces)
        first = (in_me ^ k) * length
        for piece in pieces:
            place = panel.at[pl.ds(first, piece.shape[0])]
            copies.append(pltpu.make_async_copy(piece, place, sems.at[len(copies)]))
            first = first + piece.shape[0]
    for copy in copies:
        copy.start()
    acc[...] = jnp.zeros_like(acc) if carried is None else carried[...]
    for copy in copies:
        copy.wait()

    def one_group(g, carry):
        products = []
        targets = []
        for u in range(UNROLL):
            k = g * UNROLL + u
            block = values[index[0, k]]
            piece = panel[index[1, k]]
            if forward:
                products.append(jnp.dot(block, piece, preferred_element_type=F32))
            else:
                products.append(jnp.dot(piece, block, preferred_element_type=F32))
            targets.append(index[2, k])
        for target, product in zip(targets, products):
            acc[target] += product
        return carry

    low, high = (index[3, 0], index[4, 0]) if second else (0, index[3, 0])
    lax.fori_loop(low, high, one_group, 0)


def nested(form, refs):
    refs = iter(refs)
    return [[next(refs) for _ in range(pieces)] for pieces in form]


def halves(value):
    middle = value.shape[0] // 2
    return [value[:middle], value[middle:]] if middle else [value]


def block_of(pieces, b):
    for piece in pieces:
        if b < piece.shape[0]:
            return piece[b].astype(F32)
        b -= piece.shape[0]


def early_kernel(form, early, lists, values, *refs):
    shards, out, scratch = nested(form, refs), refs[sum(form)], refs[-4:]
    product_body("row", True, False, lists, values, list(zip(early, shards)), scratch)
    out[...] = scratch[1][...]


def left_kernel(form, late, lists, values, *refs):
    *shards, (carried,) = nested(form, refs)
    outs, scratch = refs[sum(form):-4], refs[-4:]
    product_body("row", True, True, lists, values, list(zip(late, shards)), scratch, carried)
    acc = scratch[1]
    per = (acc.shape[0] - 1) // len(outs)
    me = lax.axis_index("col")
    for k in range(len(outs)):
        part = acc[pl.ds((me ^ k) * per, per)]
        outs[k][...] = part.astype(outs[k].dtype)


def right_kernel(form, second, lists, values, *refs):
    shards, out, scratch = nested(form, refs), refs[sum(form)], refs[-4:]
    product_body("col", False, second, lists, values, list(enumerate(shards)), scratch)
    acc = scratch[1]
    per = out.shape[1]
    me = lax.axis_index("row")
    for k in range(out.shape[0]):
        distance = 2 * k + (0 if second else 1)
        out[k] = acc[pl.ds((me ^ distance) * per, per)].astype(out.dtype)


def run_product(kernel, other, lists, values, shards, panel_blocks, out_blocks, out_shape, carried=()):
    slots, size = values.shape[0], values.shape[-1]
    width = shards[0][0].shape[-1]
    shards = list(shards) + [[term] for term in carried]
    form = tuple(map(len, shards))
    shards = jax.tree.leaves(shards)
    held = [
        pltpu.VMEM((panel_blocks, size, width), BF16),
        pltpu.VMEM((out_blocks + 1, size, width), F32),
    ]
    return pl.pallas_call(
        functools.partial(kernel, form, other),
        out_shape=out_shape,
        in_specs=[ANY, VMEM] + [ANY] * (len(shards) - len(carried)) + [VMEM] * len(carried),
        out_specs=jax.tree.map(lambda _: VMEM, out_shape),
        scratch_shapes=held
        + [pltpu.SMEM(lists.shape, jnp.int32), pltpu.SemaphoreType.DMA((len(shards) + 1,))],
        compiler_params=params(held + jax.tree.leaves(out_shape) + [values] + list(carried)),
        cost_estimate=pl.CostEstimate(
            flops=2 * slots * size * size * width, bytes_accessed=2 * values.size, transcendentals=0
        ),
    )(lists, values, *shards)


def bucket_lists(second, target, source, live, spare, places):
    slots = target.shape[1]
    down = lax.broadcasted_iota(jnp.int32, (slots, slots), 0)
    along = lax.broadcasted_iota(jnp.int32, (slots, slots), 1)

    def column(values):
        return jnp.sum(jnp.where(down == along, values, 0.0), axis=1, keepdims=True)

    key = jnp.where(live, jnp.where(second, 1.0, 0.0), 2.0)
    before = jnp.sum(jnp.where((column(key) == key) & (down < along), 1.0, 0.0), axis=0, keepdims=True)
    steps = [
        jnp.floor((jnp.sum(jnp.where(key == bucket, 1.0, 0.0), axis=1, keepdims=True) + (UNROLL - 1.0)) / UNROLL)
        for bucket in (0.0, 1.0)
    ]
    place = column(jnp.where(live, before + key * steps[0] * UNROLL, -1.0))
    hit = lax.broadcasted_iota(jnp.int32, (slots, places), 1).astype(F32) == place
    number = lax.broadcasted_iota(jnp.int32, (slots, 1), 0).astype(F32)

    def placed(values, default):
        return jnp.sum(jnp.where(hit, values - default, 0.0), axis=0, keepdims=True) + default

    lists = [placed(number, 0.0), placed(column(source), 0.0), placed(column(target), spare)]
    return lists + [jnp.broadcast_to(count, (1, places)) for count in (steps[0], steps[0] + steps[1])]


def stage_kernel(row_blocks, col_blocks, per, counts, rows, cols, values, left, right, staged, sem):
    copy = pltpu.make_async_copy(values.at[0, 0], staged, sem)
    copy.start()
    row, col = rows[0], cols[0]
    live = lax.broadcasted_iota(jnp.int32, row.shape, 1) < counts[0, 0]
    row_size = col_blocks // per
    distance = lax.div(col, jnp.full_like(col, per)) ^ lax.axis_index("row")
    late = distance >= row_size - 2
    kept = (distance & 1) == 0
    row, col = row.astype(F32), col.astype(F32)
    places = left.shape[1]
    for out, lists in (
        (left, bucket_lists(late, row, col, live, float(row_blocks), places)),
        (right, bucket_lists(kept, col, row, live, float(col_blocks), places)),
    ):
        for k, line in enumerate(lists):
            out[k:k + 1, :] = line.astype(jnp.int32)
    copy.wait()


def left_sum_kernel(nodes_total, own, *refs):
    parts, (natural, flipped, gram) = refs[:-3], refs[-3:]
    total = jnp.zeros(gram.shape, F32)
    for b in range(own.shape[0]):
        summed = own[b]
        for part in parts:
            summed = summed + part[b].astype(F32)
        rounded = summed.astype(BF16)
        turned = summed.T.astype(BF16)
        natural[b] = rounded
        flipped[b] = turned
        total = total + jnp.dot(turned, rounded, preferred_element_type=F32)
    gram[...] = total / nodes_total


def core_sum_kernel(form, keep, came, *outs):
    for k, pieces in enumerate(nested(form, outs)):
        first = 0
        for out in pieces:
            span = pl.ds(first, out.shape[0])
            out[...] = (keep[k, span] + came[k, span].astype(F32)).astype(out.dtype)
            first += out.shape[0]


def inverse_lower(gram):
    order = gram.shape[0]
    panels = order // STEP
    lanes = lax.broadcasted_iota(jnp.int32, (STEP, order), 1)
    strips = [gram[t * STEP:(t + 1) * STEP, :] for t in range(panels)]
    finals = []

    def column(strip, lane):
        return jnp.broadcast_to(strip[:, lane:lane + 1], strip.shape)

    def row(strip, sub):
        return jnp.broadcast_to(strip[sub:sub + 1, :], strip.shape)

    for t in range(panels):
        base = t * STEP
        strip = strips[t]
        cols = [column(strip, base + s) for s in range(STEP)]
        scales, weights, rows_done = [], [], []
        for s in range(STEP):
            scale = lax.rsqrt(row(cols[s], s))
            lower = cols[s] * scale
            scales.append(scale)
            picks = [None] * STEP
            for u in range(s + 1, STEP):
                picks[u] = row(lower, u)
                cols[u] = cols[u] - lower * picks[u]
            weights.append(picks)
            done = jnp.where(lanes == base + s, scale, row(strip, s) * scale)
            done = jnp.where((lanes > base + s) & (lanes < base + STEP), 0.0, done)
            rows_done.append(done)
            if s + 1 < STEP:
                strip = jnp.where(lanes == base + s, 0.0, strip) - lower * done
        sub = lax.broadcasted_iota(jnp.int32, (STEP, order), 0)
        final = rows_done[0]
        for s in range(1, STEP):
            final = jnp.where(sub == s, rows_done[s], final)
        finals.append(jnp.where(lanes <= base + sub, final, 0.0))
        inside = (lanes >= base) & (lanes < base + STEP)
        for v in range(t + 1, panels):
            below = strips[v]
            parts = [column(below, base + s) for s in range(STEP)]
            update = jnp.where(inside, 0.0, below)
            for s in range(STEP):
                part = parts[s] * scales[s]
                for u in range(s + 1, STEP):
                    parts[u] = parts[u] - part * weights[s][u]
                update = update - part * rows_done[s]
            strips[v] = update
    return finals


def limbs(value, depth):
    terms = []
    for _ in range(depth):
        term = value.astype(BF16)
        value = value - term.astype(F32)
        terms.append(term)
    return terms


def fold(stacked, order):
    total = stacked[-order:]
    for low in range(stacked.shape[0] - 2 * order, -1, -order):
        total = stacked[low:low + order] + total
    return total


def factor_of(parts, scratch):
    total = parts[0][...]
    for part in parts[1:]:
        total = total + part[...].astype(F32)
    for t, strip in enumerate(inverse_lower(total)):
        scratch[t * STEP:(t + 1) * STEP, :] = strip
    return scratch[...]


def right_sum_kernel(form, nodes_total, inverse, own, *refs):
    parts, (flipped, gram) = nested(form, refs), refs[-2:]
    order = inverse.shape[0]
    factor = limbs(inverse[...], 3)
    full, head = jnp.concatenate(factor, 0), jnp.concatenate(factor[:2], 0)
    total = jnp.zeros(gram.shape, F32)
    for b in range(own.shape[0]):
        summed = own[b]
        for part in parts:
            summed = summed + block_of(part, b)
        first, second = limbs(summed, 2)
        scaled = fold(jnp.dot(head, second, preferred_element_type=F32), order)
        scaled = scaled + fold(jnp.dot(full, first, preferred_element_type=F32), order)
        rounded = scaled.astype(BF16)
        flipped[b] = rounded
        total = total + lax.dot_general(rounded, rounded, (((1,), (1,)), ((), ())), preferred_element_type=F32)
    gram[...] = total / nodes_total


def left_factor_kernel(*refs):
    parts, natural, inverse, out = refs[:-3], refs[-3], refs[-2], refs[-1]
    factor = factor_of(parts, inverse)
    terms = limbs(factor, 3)
    for b in range(natural.shape[0]):
        solved = jnp.zeros(out.shape[1:], F32)
        for term in reversed(terms):
            solved = solved + lax.dot_general(
                natural[b], term, (((1,), (1,)), ((), ())), preferred_element_type=F32
            )
        out[b] = solved.astype(BF16)


def right_factor_kernel(*refs):
    parts, flipped, out, scratch = refs[:-3], refs[-3], refs[-2], refs[-1]
    factor = factor_of(parts, scratch)
    stacked = jnp.concatenate(limbs(factor, 3), 0)
    for b in range(flipped.shape[0]):
        solved = fold(jnp.dot(stacked, flipped[b], preferred_element_type=F32), factor.shape[0])
        out[b] = solved.T.astype(BF16)


def call(kernel, out_shape, *args, scratch=()):
    return pl.pallas_call(
        kernel,
        out_shape=out_shape,
        in_specs=[VMEM] * len(args),
        out_specs=jax.tree.map(lambda _: VMEM, out_shape),
        scratch_shapes=scratch,
        compiler_params=params(list(args) + jax.tree.leaves(out_shape) + list(scratch)),
    )(*args)


def shape(dims, kind):
    return jax.ShapeDtypeStruct(dims, kind)


def exchange(value, axis, first, step=1):
    sent = value.astype(BF16)
    return [value] + [swap(sent, axis, k) for k in range(first, lax.axis_size(axis), step)]


def add_parts(parts):
    return functools.reduce(lambda total, part: total + part.astype(total.dtype), parts)


def gather_row(shard):
    row_size = lax.axis_size("row")
    top = row_size // 2
    have = {0: [shard], top: [swap(piece, "row", top) for piece in halves(shard)]}
    bit = top // 2
    while bit:
        for k in sorted(have, reverse=True):
            have[k | bit] = [swap(piece, "row", bit) for piece in have[k]]
        bit //= 2
    return [have[k] for k in range(row_size)]


def collect_row(terms):
    row_size = lax.axis_size("row")
    came = []
    bit = 2
    while bit < row_size:
        for k in sorted(terms, reverse=True):
            if not k & bit:
                continue
            moved = [swap(piece.astype(BF16), "row", bit) for piece in terms.pop(k)]
            if k ^ bit:
                terms[k ^ bit] = [(a + b.astype(F32)) for a, b in zip(terms[k ^ bit], moved)]
            else:
                came.append(moved)
        bit *= 2
    return came


def local(start_panel, block_values, block_rows, block_cols, block_counts):
    group_rows, width = start_panel.shape
    row_size = lax.axis_size("row")
    col_size = lax.axis_size("col")
    nodes_total = group_rows * row_size * col_size
    size = block_values.shape[-1]
    slots = block_values.shape[2]
    per = group_rows // size
    row_blocks, col_blocks = per * col_size, per * row_size
    block = (per, size, width)
    square = shape((width, width), F32)
    places = (-(-slots // UNROLL) + 2) * UNROLL
    staged = (shape((5, places), jnp.int32),) * 2 + (shape((slots, size, size), BF16),)
    left_list, right_list, values = pl.pallas_call(
        functools.partial(stage_kernel, row_blocks, col_blocks, per),
        out_shape=staged,
        in_specs=[SMEM, VMEM, VMEM, HBM],
        out_specs=(VMEM,) * len(staged),
        scratch_shapes=[pltpu.SemaphoreType.DMA(())],
        compiler_params=params(staged),
    )(block_counts, block_rows, block_cols, block_values)

    shards = gather_row(start_panel.reshape(block))
    early, late = range(row_size - 2), range(row_size - 2, row_size)
    carried = run_product(
        early_kernel, early, left_list, values, [shards[k] for k in early], col_blocks, row_blocks,
        shape((row_blocks + 1, size, width), F32),
    )
    parts = run_product(
        left_kernel, late, left_list, values, [shards[k] for k in late], col_blocks, row_blocks,
        [shape(block, F32)] + [shape(block, BF16)] * (col_size - 1), (carried,),
    )
    came = [swap(parts[k], "col", k) for k in range(1, col_size)]
    natural, flipped, gram = call(
        functools.partial(left_sum_kernel, nodes_total),
        (shape(block, BF16), shape(block, BF16), square), parts[0], *came,
    )
    turned = exchange(flipped, "col", 1)
    gram = add_parts(exchange(gram + swap(gram, "row", 1), "row", 2, 2))
    gram, turned = lax.optimization_barrier((gram, turned))

    half = (row_size // 2,) + block
    turned = [[part] for part in turned]
    send = run_product(
        right_kernel, False, right_list, values, turned, row_blocks, col_blocks, shape(half, BF16)
    )
    returned = swap(send, "row", 1)
    keep = run_product(
        right_kernel, True, right_list, values, turned, row_blocks, col_blocks, shape(half, F32)
    )
    pieces = {0: [shape(block, F32)]}
    for k in range(2, row_size, 2):
        far = 2 if k & (row_size // 2) and per % 2 == 0 else 1
        kind = BF16 if k & 2 else F32
        pieces[k] = [shape((per // far, size, width), kind)] * far
    form = tuple(map(len, pieces.values()))
    sums = call(
        functools.partial(core_sum_kernel, form), jax.tree.leaves(list(pieces.values())), keep, returned
    )
    terms = dict(zip(pieces, nested(form, sums)))
    (own,) = terms.pop(0)
    gram, _ = lax.optimization_barrier((gram, own))
    came = collect_row(terms)
    grams = exchange(gram, "col", 1)
    inverse, left_panel = call(left_factor_kernel, (square, shape(block, BF16)), *grams, natural)
    right_flipped, gram = call(
        functools.partial(right_sum_kernel, tuple(map(len, came)), nodes_total),
        (shape(block, BF16), square), inverse, own, *jax.tree.leaves(came),
    )
    gram = gram + swap(gram, "row", 1)
    gram = add_parts(exchange(gram, "col", 1))
    right_panel = call(
        right_factor_kernel, shape(block, BF16), *exchange(gram, "row", 2, 2), right_flipped,
        scratch=[pltpu.VMEM((width, width), F32)],
    )
    return (left_panel.reshape(group_rows, width), right_panel.reshape(group_rows, width))


def solution(mesh):
    return jax.shard_map(
        local,
        mesh=mesh,
        in_specs=(
            P(("col", "row"), None),
            P("row", "col", None, None, None),
            P("row", "col", None),
            P("row", "col", None),
            P("row", "col"),
        ),
        out_specs=(P(("row", "col"), None), P(("col", "row"), None)),
        check_vma=False,
    )
```

```python
import functools

import jax
import jax.numpy as jnp
from jax import lax
from jax.experimental import pallas as pl
from jax.experimental.pallas import tpu as pltpu
from jax.sharding import PartitionSpec as P


F32 = jnp.float32
BF16 = jnp.bfloat16
UNROLL = 32
STEP = 8
MARGIN = 4 * 1024 * 1024
VMEM = pl.BlockSpec(memory_space=pltpu.VMEM)
SMEM = pl.BlockSpec(memory_space=pltpu.SMEM)
ANY = pl.BlockSpec(memory_space=pl.ANY)
HBM = pl.BlockSpec(memory_space=pltpu.HBM)


def nbytes(item):
    total = jnp.dtype(item.dtype).itemsize
    for extent in item.shape:
        total *= extent
    return total


def params(items):
    return pltpu.CompilerParams(vmem_limit_bytes=sum(map(nbytes, items)) + MARGIN)


def swap(value, axis, mask):
    size = lax.axis_size(axis)
    return lax.ppermute(value, axis, [(i, i ^ mask) for i in range(size)])


def product_body(in_axis, forward, second, lists, values, shards, scratch, carried=None):
    in_me = lax.axis_index(in_axis)
    panel, acc, index, sems = scratch
    copies = [pltpu.make_async_copy(lists, index, sems.at[0])]
    for k, pieces in shards:
        length = sum(piece.shape[0] for piece in pieces)
        first = (in_me ^ k) * length
        for piece in pieces:
            place = panel.at[pl.ds(first, piece.shape[0])]
            copies.append(pltpu.make_async_copy(piece, place, sems.at[len(copies)]))
            first = first + piece.shape[0]
    for copy in copies:
        copy.start()
    acc[...] = jnp.zeros_like(acc) if carried is None else carried[...]
    for copy in copies:
        copy.wait()

    def one_group(g, carry):
        products = []
        targets = []
        for u in range(UNROLL):
            k = g * UNROLL + u
            block = values[index[0, k]]
            piece = panel[index[1, k]]
            if forward:
                products.append(jnp.dot(block, piece, preferred_element_type=F32))
            else:
                products.append(jnp.dot(piece, block, preferred_element_type=F32))
            targets.append(index[2, k])
        for target, product in zip(targets, products):
            acc[target] += product
        return carry

    low, high = (index[3, 0], index[4, 0]) if second else (0, index[3, 0])
    lax.fori_loop(low, high, one_group, 0)


def nested(form, refs):
    refs = iter(refs)
    return [[next(refs) for _ in range(pieces)] for pieces in form]


def halves(value):
    middle = value.shape[0] // 2
    return [value[:middle], value[middle:]] if middle else [value]


def block_of(pieces, b):
    for piece in pieces:
        if b < piece.shape[0]:
            return piece[b].astype(F32)
        b -= piece.shape[0]


def early_kernel(form, early, lists, values, *refs):
    shards, out, scratch = nested(form, refs), refs[sum(form)], refs[-4:]
    product_body("row", True, False, lists, values, list(zip(early, shards)), scratch)
    out[...] = scratch[1][...]


def left_kernel(form, late, lists, values, *refs):
    *shards, (carried,) = nested(form, refs)
    outs, scratch = refs[sum(form):-4], refs[-4:]
    product_body("row", True, True, lists, values, list(zip(late, shards)), scratch, carried)
    acc = scratch[1]
    per = (acc.shape[0] - 1) // len(outs)
    me = lax.axis_index("col")
    for k in range(len(outs)):
        part = acc[pl.ds((me ^ k) * per, per)]
        outs[k][...] = part.astype(outs[k].dtype)


def right_kernel(form, second, lists, values, *refs):
    shards, out, scratch = nested(form, refs), refs[sum(form)], refs[-4:]
    product_body("col", False, second, lists, values, list(enumerate(shards)), scratch)
    acc = scratch[1]
    per = out.shape[1]
    me = lax.axis_index("row")
    for k in range(out.shape[0]):
        distance = 2 * k + (0 if second else 1)
        out[k] = acc[pl.ds((me ^ distance) * per, per)].astype(out.dtype)


def run_product(kernel, other, lists, values, shards, panel_blocks, out_blocks, out_shape, carried=()):
    slots, size = values.shape[0], values.shape[-1]
    width = shards[0][0].shape[-1]
    shards = list(shards) + [[term] for term in carried]
    form = tuple(map(len, shards))
    shards = jax.tree.leaves(shards)
    held = [
        pltpu.VMEM((panel_blocks, size, width), BF16),
        pltpu.VMEM((out_blocks + 1, size, width), F32),
    ]
    return pl.pallas_call(
        functools.partial(kernel, form, other),
        out_shape=out_shape,
        in_specs=[ANY, VMEM] + [ANY] * (len(shards) - len(carried)) + [VMEM] * len(carried),
        out_specs=jax.tree.map(lambda _: VMEM, out_shape),
        scratch_shapes=held
        + [pltpu.SMEM(lists.shape, jnp.int32), pltpu.SemaphoreType.DMA((len(shards) + 1,))],
        compiler_params=params(held + jax.tree.leaves(out_shape) + [values] + list(carried)),
        cost_estimate=pl.CostEstimate(
            flops=2 * slots * size * size * width, bytes_accessed=2 * values.size, transcendentals=0
        ),
    )(lists, values, *shards)


def bucket_lists(second, target, source, live, spare, places):
    slots = target.shape[1]
    down = lax.broadcasted_iota(jnp.int32, (slots, slots), 0)
    along = lax.broadcasted_iota(jnp.int32, (slots, slots), 1)

    def column(values):
        return jnp.sum(jnp.where(down == along, values, 0.0), axis=1, keepdims=True)

    key = jnp.where(live, jnp.where(second, 1.0, 0.0), 2.0)
    before = jnp.sum(jnp.where((column(key) == key) & (down < along), 1.0, 0.0), axis=0, keepdims=True)
    steps = [
        jnp.floor((jnp.sum(jnp.where(key == bucket, 1.0, 0.0), axis=1, keepdims=True) + (UNROLL - 1.0)) / UNROLL)
        for bucket in (0.0, 1.0)
    ]
    place = column(jnp.where(live, before + key * steps[0] * UNROLL, -1.0))
    hit = lax.broadcasted_iota(jnp.int32, (slots, places), 1).astype(F32) == place
    number = lax.broadcasted_iota(jnp.int32, (slots, 1), 0).astype(F32)

    def placed(values, default):
        return jnp.sum(jnp.where(hit, values - default, 0.0), axis=0, keepdims=True) + default

    lists = [placed(number, 0.0), placed(column(source), 0.0), placed(column(target), spare)]
    return lists + [jnp.broadcast_to(count, (1, places)) for count in (steps[0], steps[0] + steps[1])]


def stage_kernel(row_blocks, col_blocks, per, counts, rows, cols, values, left, right, staged, sem):
    copy = pltpu.make_async_copy(values.at[0, 0], staged, sem)
    copy.start()
    row, col = rows[0], cols[0]
    live = lax.broadcasted_iota(jnp.int32, row.shape, 1) < counts[0, 0]
    row_size = col_blocks // per
    distance = lax.div(col, jnp.full_like(col, per)) ^ lax.axis_index("row")
    late = distance >= row_size - 2
    kept = (distance & 1) == 0
    row, col = row.astype(F32), col.astype(F32)
    places = left.shape[1]
    for out, lists in (
        (left, bucket_lists(late, row, col, live, float(row_blocks), places)),
        (right, bucket_lists(kept, col, row, live, float(col_blocks), places)),
    ):
        for k, line in enumerate(lists):
            out[k:k + 1, :] = line.astype(jnp.int32)
    copy.wait()


def left_sum_kernel(nodes_total, own, *refs):
    parts, (natural, flipped, gram) = refs[:-3], refs[-3:]
    total = jnp.zeros(gram.shape, F32)
    for b in range(own.shape[0]):
        summed = own[b]
        for part in parts:
            summed = summed + part[b].astype(F32)
        rounded = summed.astype(BF16)
        turned = summed.T.astype(BF16)
        natural[b] = rounded
        flipped[b] = turned
        total = total + jnp.dot(turned, rounded, preferred_element_type=F32)
    gram[...] = total / nodes_total


def core_sum_kernel(form, keep, came, *outs):
    for k, pieces in enumerate(nested(form, outs)):
        first = 0
        for out in pieces:
            span = pl.ds(first, out.shape[0])
            out[...] = (keep[k, span] + came[k, span].astype(F32)).astype(out.dtype)
            first += out.shape[0]


def inverse_lower(gram):
    order = gram.shape[0]
    panels = order // STEP
    lanes = lax.broadcasted_iota(jnp.int32, (STEP, order), 1)
    strips = [gram[t * STEP:(t + 1) * STEP, :] for t in range(panels)]
    finals = []

    def column(strip, lane):
        return jnp.broadcast_to(strip[:, lane:lane + 1], strip.shape)

    def row(strip, sub):
        return jnp.broadcast_to(strip[sub:sub + 1, :], strip.shape)

    for t in range(panels):
        base = t * STEP
        strip = strips[t]
        cols = [column(strip, base + s) for s in range(STEP)]
        scales, weights, rows_done = [], [], []
        for s in range(STEP):
            scale = lax.rsqrt(row(cols[s], s))
            lower = cols[s] * scale
            scales.append(scale)
            picks = [None] * STEP
            for u in range(s + 1, STEP):
                picks[u] = row(lower, u)
                cols[u] = cols[u] - lower * picks[u]
            weights.append(picks)
            done = jnp.where(lanes == base + s, scale, row(strip, s) * scale)
            done = jnp.where((lanes > base + s) & (lanes < base + STEP), 0.0, done)
            rows_done.append(done)
            if s + 1 < STEP:
                strip = jnp.where(lanes == base + s, 0.0, strip) - lower * done
        sub = lax.broadcasted_iota(jnp.int32, (STEP, order), 0)
        final = rows_done[0]
        for s in range(1, STEP):
            final = jnp.where(sub == s, rows_done[s], final)
        finals.append(jnp.where(lanes <= base + sub, final, 0.0))
        inside = (lanes >= base) & (lanes < base + STEP)
        for v in range(t + 1, panels):
            below = strips[v]
            parts = [column(below, base + s) for s in range(STEP)]
            update = jnp.where(inside, 0.0, below)
            for s in range(STEP):
                part = parts[s] * scales[s]
                for u in range(s + 1, STEP):
                    parts[u] = parts[u] - part * weights[s][u]
                update = update - part * rows_done[s]
            strips[v] = update
    return finals


def limbs(value, depth):
    terms = []
    for _ in range(depth):
        term = value.astype(BF16)
        value = value - term.astype(F32)
        terms.append(term)
    return terms


def fold(stacked, order):
    total = stacked[-order:]
    for low in range(stacked.shape[0] - 2 * order, -1, -order):
        total = stacked[low:low + order] + total
    return total


def factor_of(parts, scratch):
    total = parts[0][...]
    for part in parts[1:]:
        total = total + part[...].astype(F32)
    for t, strip in enumerate(inverse_lower(total)):
        scratch[t * STEP:(t + 1) * STEP, :] = strip
    return scratch[...]


def right_sum_kernel(form, nodes_total, inverse, own, *refs):
    parts, (flipped, gram) = nested(form, refs), refs[-2:]
    order = inverse.shape[0]
    factor = limbs(inverse[...], 3)
    full, head = jnp.concatenate(factor, 0), jnp.concatenate(factor[:2], 0)
    total = jnp.zeros(gram.shape, F32)
    for b in range(own.shape[0]):
        summed = own[b]
        for part in parts:
            summed = summed + block_of(part, b)
        first, second = limbs(summed, 2)
        scaled = fold(jnp.dot(head, second, preferred_element_type=F32), order)
        scaled = scaled + fold(jnp.dot(full, first, preferred_element_type=F32), order)
        rounded = scaled.astype(BF16)
        flipped[b] = rounded
        total = total + lax.dot_general(rounded, rounded, (((1,), (1,)), ((), ())), preferred_element_type=F32)
    gram[...] = total / nodes_total


def left_factor_kernel(*refs):
    parts, natural, inverse, out = refs[:-3], refs[-3], refs[-2], refs[-1]
    factor = factor_of(parts, inverse)
    terms = limbs(factor, 3)
    for b in range(natural.shape[0]):
        solved = jnp.zeros(out.shape[1:], F32)
        for term in reversed(terms):
            solved = solved + lax.dot_general(
                natural[b], term, (((1,), (1,)), ((), ())), preferred_element_type=F32
            )
        out[b] = solved.astype(BF16)


def right_factor_kernel(*refs):
    parts, flipped, out, scratch = refs[:-3], refs[-3], refs[-2], refs[-1]
    factor = factor_of(parts, scratch)
    stacked = jnp.concatenate(limbs(factor, 3), 0)
    for b in range(flipped.shape[0]):
        solved = fold(jnp.dot(stacked, flipped[b], preferred_element_type=F32), factor.shape[0])
        out[b] = solved.T.astype(BF16)


def call(kernel, out_shape, *args, scratch=()):
    return pl.pallas_call(
        kernel,
        out_shape=out_shape,
        in_specs=[VMEM] * len(args),
        out_specs=jax.tree.map(lambda _: VMEM, out_shape),
        scratch_shapes=scratch,
        compiler_params=params(list(args) + jax.tree.leaves(out_shape) + list(scratch)),
    )(*args)


def shape(dims, kind):
    return jax.ShapeDtypeStruct(dims, kind)


def exchange(value, axis, first, step=1):
    sent = value.astype(BF16)
    return [value] + [swap(sent, axis, k) for k in range(first, lax.axis_size(axis), step)]


def add_parts(parts):
    return functools.reduce(lambda total, part: total + part.astype(total.dtype), parts)


def gather_row(shard):
    row_size = lax.axis_size("row")
    top = row_size // 2
    have = {0: [shard], top: [swap(piece, "row", top) for piece in halves(shard)]}
    bit = top // 2
    while bit:
        for k in sorted(have, reverse=True):
            have[k | bit] = [swap(piece, "row", bit) for piece in have[k]]
        bit //= 2
    return [have[k] for k in range(row_size)]


def collect_row(terms):
    row_size = lax.axis_size("row")
    came = []
    bit = 2
    while bit < row_size:
        for k in sorted(terms, reverse=True):
            if not k & bit:
                continue
            moved = [swap(piece.astype(BF16), "row", bit) for piece in terms.pop(k)]
            if k ^ bit:
                terms[k ^ bit] = [(a + b.astype(F32)) for a, b in zip(terms[k ^ bit], moved)]
            else:
                came.append(moved)
        bit *= 2
    return came


def local(start_panel, block_values, block_rows, block_cols, block_counts):
    group_rows, width = start_panel.shape
    row_size = lax.axis_size("row")
    col_size = lax.axis_size("col")
    nodes_total = group_rows * row_size * col_size
    size = block_values.shape[-1]
    slots = block_values.shape[2]
    per = group_rows // size
    row_blocks, col_blocks = per * col_size, per * row_size
    block = (per, size, width)
    square = shape((width, width), F32)
    places = (-(-slots // UNROLL) + 2) * UNROLL
    staged = (shape((5, places), jnp.int32),) * 2 + (shape((slots, size, size), BF16),)
    left_list, right_list, values = pl.pallas_call(
        functools.partial(stage_kernel, row_blocks, col_blocks, per),
        out_shape=staged,
        in_specs=[SMEM, VMEM, VMEM, HBM],
        out_specs=(VMEM,) * len(staged),
        scratch_shapes=[pltpu.SemaphoreType.DMA(())],
        compiler_params=params(staged),
    )(block_counts, block_rows, block_cols, block_values)

    shards = gather_row(start_panel.reshape(block))
    early, late = range(row_size - 2), range(row_size - 2, row_size)
    carried = run_product(
        early_kernel, early, left_list, values, [shards[k] for k in early], col_blocks, row_blocks,
        shape((row_blocks + 1, size, width), F32),
    )
    parts = run_product(
        left_kernel, late, left_list, values, [shards[k] for k in late], col_blocks, row_blocks,
        [shape(block, F32)] + [shape(block, BF16)] * (col_size - 1), (carried,),
    )
    came = [swap(parts[k], "col", k) for k in range(1, col_size)]
    natural, flipped, gram = call(
        functools.partial(left_sum_kernel, nodes_total),
        (shape(block, BF16), shape(block, BF16), square), parts[0], *came,
    )
    turned = exchange(flipped, "col", 1)
    gram = add_parts(exchange(gram + swap(gram, "row", 1), "row", 2, 2))
    gram, turned = lax.optimization_barrier((gram, turned))

    half = (row_size // 2,) + block
    turned = [[part] for part in turned]
    send = run_product(
        right_kernel, False, right_list, values, turned, row_blocks, col_blocks, shape(half, BF16)
    )
    returned = swap(send, "row", 1)
    keep = run_product(
        right_kernel, True, right_list, values, turned, row_blocks, col_blocks, shape(half, F32)
    )
    pieces = {0: [shape(block, F32)]}
    for k in range(2, row_size, 2):
        far = 2 if k & (row_size // 2) and per % 2 == 0 else 1
        kind = BF16 if k & 2 else F32
        pieces[k] = [shape((per // far, size, width), kind)] * far
    form = tuple(map(len, pieces.values()))
    sums = call(
        functools.partial(core_sum_kernel, form), jax.tree.leaves(list(pieces.values())), keep, returned
    )
    terms = dict(zip(pieces, nested(form, sums)))
    (own,) = terms.pop(0)
    gram, _ = lax.optimization_barrier((gram, own))
    came = collect_row(terms)
    grams = exchange(gram, "col", 1)
    inverse, left_panel = call(left_factor_kernel, (square, shape(block, BF16)), *grams, natural)
    right_flipped, gram = call(
        functools.partial(right_sum_kernel, tuple(map(len, came)), nodes_total),
        (shape(block, BF16), square), inverse, own, *jax.tree.leaves(came),
    )
    gram = gram + swap(gram, "row", 1)
    hops = [("col", 1 << b) for b in range((col_size - 1).bit_length())]
    hops += [("row", 1 << b) for b in range(1, (row_size - 1).bit_length())]
    for axis, mask in hops[:-1]:
        gram = add_parts([gram, swap(gram.astype(BF16), axis, mask)])
    last = [gram, swap(gram.astype(BF16), *hops[-1])]
    right_panel = call(
        right_factor_kernel, shape(block, BF16), *last, right_flipped,
        scratch=[pltpu.VMEM((width, width), F32)],
    )
    return (left_panel.reshape(group_rows, width), right_panel.reshape(group_rows, width))


def solution(mesh):
    return jax.shard_map(
        local,
        mesh=mesh,
        in_specs=(
            P(("col", "row"), None),
            P("row", "col", None, None, None),
            P("row", "col", None),
            P("row", "col", None),
            P("row", "col"),
        ),
        out_specs=(P(("row", "col"), None), P(("col", "row"), None)),
        check_vma=False,
    )
```
